32 devices in a mesh: tile: 16 (over z, y, x), gene: 2 (over core).
Axes of the slice: x: 2, y: 2, z: 4, core: 2. Of those that a mesh axis runs over, the one named last changes fastest.
Arguments:
- source_expr: bfloat16 [2000, 49152], P('gene', 'tile'), may hold values from -6 to 6
- target_expr: bfloat16 [2000, 49152], P('gene', 'tile'), may hold values from -6 to 6
- prior_plan: bfloat16 [384, 8, 128, 128], P('tile'), may hold values from 0.01 to 46
- nonzero_pattern: int32 [384, 8], P('tile'), may hold values from 0 to 383, as said below
- live: int32 [384], P('tile'), may hold values from 1 to 8, as said below
- source_mass: float32 [49152], P('tile'), may hold values from 0.2 to 5
- target_mass: float32 [49152], P('tile'), may hold values from 0.2 to 5
- initial_logarithm_right: float32 [49152], P('tile'), may hold values from -4 to 263
Outputs:
- logarithm_left_factors: float32 [49152], P('tile')
- logarithm_right_factors: float32 [49152], P('tile')
The draws below stay inside these ranges and needn't reach their ends.
Inputs may be any that keep to these rules, and one draw needn't show every extreme that they name: nonzero_pattern[n, 0] is n; the other entries of row n are distinct bins, none equal to n, of the tile of bin n or of an adjacent tile (bin n lies in tile n div 24). Some source bin has all 8 blocks live.
All inputs are finite; a program needn't handle non-finite values.
Results may differ from the reference program's by a relative error of at most 0.0003.
Values may be sent and summed in bfloat16 or wider, within the bound.
A program may use at most 192 MiB of HBM per device.

```python
import math
import jax
import jax.numpy as jnp
from jax import lax

G = 2000
UNITS_IN_GROUP = 128
BINS_DEV = 24
SLOTS = 8
ITERS = 3
SLICE_GROUPS = 384
NCELLS = 49152


def draw_prior_plan(key, part):
    first, second = jax.random.split(key)
    scale = jnp.exp(jax.random.uniform(first, (SLICE_GROUPS, 1, 1, 1), jnp.float32, -2.3, 2.3))
    entry = jnp.exp(jax.random.uniform(second, (SLICE_GROUPS, SLOTS, UNITS_IN_GROUP, UNITS_IN_GROUP), jnp.float32, -0.7, 0.7))
    return (scale * entry).astype(jnp.bfloat16)


def draw_nonzero_pattern(key, part):
    span = 3 * BINS_DEV
    bins = jnp.arange(SLICE_GROUPS, dtype=jnp.int32)
    tiles = bins // BINS_DEV
    offset = jnp.arange(span, dtype=jnp.int32)
    cand = (tiles[:, None] - 1) * BINS_DEV + offset[None, :]
    invalid = (cand < 0) | (cand >= SLICE_GROUPS) | (cand == bins[:, None])
    scores = jax.random.randint(key, (SLICE_GROUPS, span), 0, 2 ** 20) * span + offset[None, :]
    ranked = scores + invalid.astype(jnp.int32) * 2 ** 29
    order = jnp.argsort(ranked, axis=1)
    picked = jnp.take_along_axis(cand, order[:, :SLOTS - 1], axis=1)
    return jnp.concatenate([bins[:, None], picked], axis=1).astype(jnp.int32)


def draw_live(key, part):
    first, second, third = jax.random.split(key, 3)
    tiles = SLICE_GROUPS // BINS_DEV
    depth = jax.random.randint(first, (tiles,), SLOTS // 2, SLOTS + 1)
    bins = jnp.arange(SLICE_GROUPS, dtype=jnp.int32)
    count = 1 + jax.random.randint(second, (SLICE_GROUPS,), 0, 2 ** 20) % depth[bins // BINS_DEV]
    chosen = jax.random.randint(third, (), 0, SLICE_GROUPS)
    return jnp.where(bins == chosen, SLOTS, count).astype(jnp.int32)


def draw_initial_logarithm_right(key, part):
    first = jax.random.fold_in(key, 0)
    return jnp.clip(jax.random.normal(first, (SLICE_GROUPS * UNITS_IN_GROUP,), jnp.float32), -4.0, 4.0)


def shard_levels(key, extent, cuts, smallest, top_value):
    def one(position, blocks):
        heights = jax.random.uniform(jax.random.fold_in(jax.random.fold_in(key, 6), position), (blocks,), jnp.float32, smallest / len(cuts), top_value / len(cuts))
        return jnp.repeat(jnp.exp(heights), extent[position] // blocks).reshape((-1,) + (1,) * (len(extent) - position - 1))

    factor_of = one(*cuts[0])
    for cut in cuts[1:]:
        factor_of = factor_of * one(*cut)
    return factor_of


def gaussian(stream_key, dims, spread, reach, cuts=(), held_as=jnp.bfloat16):
    drawn = spread * jax.random.normal(stream_key, dims, jnp.float32)
    if cuts:
        drawn = drawn * shard_levels(stream_key, dims, cuts, -0.22, 0.18)
    return jnp.clip(drawn, -reach, reach).astype(held_as)


def setup_inputs(seed: int = 0) -> dict:
    key_of = jax.random.split(jax.random.key(seed), 9)
    return {
        "source_expr": gaussian(key_of[0], (G, NCELLS), 1.0, 6.0, ((0, 2), (1, 16))),
        "target_expr": gaussian(key_of[1], (G, NCELLS), 1.0, 6.0, ((0, 2), (1, 16))),
        "prior_plan": draw_prior_plan(jax.random.fold_in(key_of[8], 71), 0),
        "nonzero_pattern": draw_nonzero_pattern(jax.random.fold_in(key_of[8], 71), 0),
        "live": draw_live(jax.random.fold_in(key_of[8], 71), 0),
        "source_mass": jnp.clip(jnp.exp(math.log(5.0) - 3.218876 * jax.random.uniform(key_of[5], (NCELLS,), jnp.float32) ** shard_levels(key_of[5], (NCELLS,), ((0, 16),), -0.2, 0.2)), 0.2, 5.0),
        "target_mass": jnp.clip(jnp.exp(math.log(5.0) - 3.218876 * jax.random.uniform(key_of[6], (NCELLS,), jnp.float32) ** shard_levels(key_of[6], (NCELLS,), ((0, 16),), -0.2, 0.2)), 0.2, 5.0),
        "initial_logarithm_right": draw_initial_logarithm_right(jax.random.fold_in(key_of[8], 71), 0),
    }


EPS = 0.02
THETA = 0.1
MINUS_HUGE = -1e30


def place_rows(bins, nbins):
    cell = jnp.arange(UNITS_IN_GROUP, dtype=jnp.int32)
    along = ((cell % 16).astype(jnp.float32) + 0.5) / 16.0
    xpos = (bins[..., None].astype(jnp.float32) + along) / nbins
    ypos = jnp.broadcast_to(((cell // 16).astype(jnp.float32) + 0.5) / (16.0 * nbins), xpos.shape)
    radius = xpos * xpos + ypos * ypos
    ones = jnp.ones_like(xpos)
    moment_rows = jnp.stack([ones, radius, xpos, ypos], axis=-1)
    dist_rows = jnp.stack([radius, ones, -2.0 * xpos, -2.0 * ypos], axis=-1)
    return moment_rows, dist_rows


def reference(source_expr, target_expr, prior_plan, nonzero_pattern, live, source_mass, target_mass, initial_logarithm_right):
    hi = lax.Precision.HIGHEST
    bins = jnp.arange(SLICE_GROUPS, dtype=jnp.int32)
    u_mom, u_dist = place_rows(bins, SLICE_GROUPS)
    v_mom = u_mom[nonzero_pattern]
    v_dist = u_dist[nonzero_pattern]
    alive_indicator = jnp.arange(SLOTS, dtype=jnp.int32)[None, :] < live[:, None]
    live_weight = alive_indicator.astype(jnp.float32)

    def block_moments(args):
        plan, urow, vrow, weight = args
        plan_f = plan.astype(jnp.float32) * weight[:, None, None]
        pv = jnp.einsum('kij,kjd->kid', plan_f, vrow, precision=hi)
        return jnp.einsum('ic,kid->cd', urow, pv, precision=hi)

    moments = jnp.sum(lax.map(block_moments, (prior_plan, u_mom, v_mom, live_weight)), axis=0)
    scaled = moments / moments[0, 0]
    target_bins = target_expr.reshape(G, SLICE_GROUPS, UNITS_IN_GROUP)

    def block_cost(args):
        index, targets, udist, vdist = args
        block = lax.dynamic_slice_in_dim(source_expr, (index * UNITS_IN_GROUP).astype(jnp.int32), UNITS_IN_GROUP, 1).astype(jnp.float32)
        chosen = jnp.take(target_bins, targets, axis=1).astype(jnp.float32)
        inner = jnp.einsum('gi,gkj->kij', block, chosen)
        left = jnp.dot(udist, scaled, precision=hi)
        gw = jnp.einsum('id,kjd->kij', left, vdist, precision=hi)
        return -inner / G + THETA * gw

    coupling_price = lax.map(block_cost, (bins, nonzero_pattern, u_dist, v_dist))
    logarithm_left_masses = jnp.log(source_mass).reshape(SLICE_GROUPS, UNITS_IN_GROUP)
    logarithm_marginal_right = jnp.log(target_mass)
    logarithm_right_factors = initial_logarithm_right
    logarithm_left_factors = jnp.zeros((SLICE_GROUPS, UNITS_IN_GROUP), jnp.float32)
    flat_targets = nonzero_pattern.reshape(-1)
    for step in range(ITERS):
        picked_right_factors = logarithm_right_factors.reshape(SLICE_GROUPS, UNITS_IN_GROUP)[nonzero_pattern]

        def left_line_panel(args):
            cb, vb, lm = args
            rating_value = jnp.where(lm[:, None, None], vb[:, None, :] - cb / EPS, MINUS_HUGE)
            top = jnp.max(rating_value, axis=(0, 2))
            return top + jnp.log(jnp.sum(jnp.exp(rating_value - top[None, :, None]), axis=(0, 2)))

        logarithm_left_factors = logarithm_left_masses - lax.map(left_line_panel, (coupling_price, picked_right_factors, alive_indicator))

        def column_panel(args):
            cb, ub, lm = args
            rating_value = jnp.where(lm[:, None, None], ub[None, :, None] - cb / EPS, MINUS_HUGE)
            top = jnp.max(rating_value, axis=1)
            grand_aggregate = jnp.sum(jnp.exp(rating_value - top[:, None, :]), axis=1)
            return top, jnp.where(lm[:, None], grand_aggregate, 0.0)

        maxima_list, aggregate_list = lax.map(column_panel, (coupling_price, logarithm_left_factors, alive_indicator))
        maxima_list = maxima_list.reshape(SLICE_GROUPS * SLOTS, UNITS_IN_GROUP)
        aggregate_list = aggregate_list.reshape(SLICE_GROUPS * SLOTS, UNITS_IN_GROUP)
        largest_found = jax.ops.segment_max(maxima_list, flat_targets, num_segments=SLICE_GROUPS)
        accumulated = jax.ops.segment_sum(aggregate_list * jnp.exp(maxima_list - largest_found[flat_targets]), flat_targets, num_segments=SLICE_GROUPS)
        logarithm_right_factors = logarithm_marginal_right - (largest_found + jnp.log(accumulated)).reshape(-1)
    return logarithm_left_factors.reshape(-1), logarithm_right_factors
```

```python
import functools

import jax
import jax.numpy as jnp
from jax import lax
from jax.experimental import pallas as pl
from jax.experimental.pallas import tpu as pltpu
from jax.sharding import PartitionSpec as P

G = 2000
ITERS = 3


EPS = 0.02
THETA = 0.1
MINUS_HUGE = -1e30


def with_halo(block, sides, width):
    for axis, dim in sides:
        count = lax.axis_size(axis)
        forward = [(i, i + 1) for i in range(count - 1)]
        backward = [(target, source) for source, target in forward]
        low = lax.ppermute(
            lax.slice_in_dim(block, block.shape[dim] - width, None, axis=dim), axis, forward
        )
        high = lax.ppermute(lax.slice_in_dim(block, 0, width, axis=dim), axis, backward)
        block = jnp.concatenate([low, block, high], axis=dim)
    return block


def place_rows(bins, nbins, spot_items):
    cell = jnp.arange(spot_items, dtype=jnp.int32)
    along = ((cell % 16).astype(jnp.float32) + 0.5) / 16.0
    xpos = (bins[..., None].astype(jnp.float32) + along) / nbins
    ypos = jnp.broadcast_to(((cell // 16).astype(jnp.float32) + 0.5) / (16.0 * nbins), xpos.shape)
    radius = xpos * xpos + ypos * ypos
    ones = jnp.ones_like(xpos)
    moment_rows = jnp.stack([ones, radius, xpos, ypos], axis=-1)
    dist_rows = jnp.stack([radius, ones, -2.0 * xpos, -2.0 * ypos], axis=-1)
    return (moment_rows, dist_rows)


def block_moments(args):
    plan, urow, vrow, weight = args
    plan_f = plan.astype(jnp.float32) * weight[:, None, None]
    pv = jnp.einsum("kij,kjd->kid", plan_f, vrow, precision=lax.Precision.HIGHEST)
    return jnp.einsum("ic,kid->cd", urow, pv, precision=lax.Precision.HIGHEST)


GROUP = 4
SEND_ROWS = 64
MESH = pl.DeviceIdType.MESH
VMEM_LIMIT = 60 * 1024 * 1024


def cuts_of(total, size):
    return [(at, min(size, total - at)) for at in range(0, total, size)]


def slot_of(rank, relative):
    low = jnp.where(rank == 0, 3, jnp.where(rank == 2, 2, 1))
    high = jnp.where(rank == 3, 3, jnp.where(rank == 1, 2, 1))
    return jnp.where(relative == 1, 0, jnp.where(relative == 0, low, high))


def halo_kernel(tiles, genes, tgt, held, send_sem, recv_sem):
    me = lax.axis_index("tile")
    rank = lax.rem(me, GROUP)
    across = {"tile": me + 1 - 2 * lax.rem(me, 2)}
    beside = {"tile": me + 2 - 4 * lax.rem(me // 2, 2)}
    edge = (rank == 0) | (rank == GROUP - 1)
    up = edge & (me + GROUP < tiles)
    down = edge & (me - GROUP >= 0)
    passes = ((rank == 0) & up) | ((rank == GROUP - 1) & down)
    gets = ((rank == 0) & down) | ((rank == GROUP - 1) & up)
    onward = {"tile": jnp.where(passes, jnp.where(rank == 0, me + GROUP, me - GROUP), me + 1 - 2 * lax.rem(me, 2))}

    barrier = pltpu.get_barrier_semaphore()
    pl.semaphore_signal(barrier, inc=1, device_id=across, device_id_type=MESH)
    pl.semaphore_signal(barrier, inc=1, device_id=beside, device_id_type=MESH)

    @pl.when(up)
    def _():
        pl.semaphore_signal(barrier, inc=1, device_id={"tile": me + GROUP}, device_id_type=MESH)

    @pl.when(down)
    def _():
        pl.semaphore_signal(barrier, inc=1, device_id={"tile": me - GROUP}, device_id_type=MESH)

    pl.semaphore_wait(barrier, 2 + up.astype(jnp.int32) + down.astype(jnp.int32))

    sends = cuts_of(genes, SEND_ROWS)

    def place(number, slot):
        at, rows = sends[number]
        return held.at[slot, pl.ds(at, rows), :]

    def copy(number, hop):
        at, rows = sends[number]
        return pltpu.make_async_remote_copy(
            src_ref=tgt.at[pl.ds(at, rows), :] if hop == 0 else place(number, hop - 1),
            dst_ref=place(number, hop),
            send_sem=send_sem.at[number, hop],
            recv_sem=recv_sem.at[number, hop],
            device_id=(across, beside, onward)[hop],
            device_id_type=MESH,
        )

    count = len(sends)
    for number in range(count):
        copy(number, 0).start()
    for step in range(count + 1):
        if step < count:
            copy(step, 0).wait_recv()
            copy(step, 1).start()
        if step >= 1:
            copy(step - 1, 1).wait_recv()

            @pl.when(passes)
            def _(step=step):
                copy(step - 1, 2).start()

    @pl.when(gets)
    def _():
        for number in range(count):
            copy(number, 2).wait_recv()

    for number in range(count):
        copy(number, 0).wait_send()
        copy(number, 1).wait_send()

    @pl.when(passes)
    def _():
        for number in range(count):
            copy(number, 2).wait_send()


def halo_of(target_expr, tiles):
    genes, width = target_expr.shape
    count = len(cuts_of(genes, SEND_ROWS))
    return pl.pallas_call(
        functools.partial(halo_kernel, tiles, genes),
        out_shape=jax.ShapeDtypeStruct((3, genes, width), target_expr.dtype),
        in_specs=[pl.BlockSpec(memory_space=pl.ANY)],
        out_specs=pl.BlockSpec(memory_space=pl.ANY),
        scratch_shapes=[pltpu.SemaphoreType.DMA((count, 3)), pltpu.SemaphoreType.DMA((count, 3))],
        compiler_params=pltpu.CompilerParams(collective_id=0, has_side_effects=True),
    )(target_expr)


def products_kernel(bins, slots, cells, live, buffers, columns, src, own, held, out):
    first = pl.program_id(0) == 0

    def one_bin(position, carry):
        block = src[:, pl.ds(pl.multiple_of(position * cells, cells), cells)]

        def one_slot(slot, inner_carry):
            number = position * slots + slot
            column = pl.ds(pl.multiple_of(columns[number], cells), cells)

            def add(other):
                part = lax.dot_general(
                    block, other, (((0,), (0,)), ((), ())), preferred_element_type=jnp.float32
                )

                @pl.when(first)
                def _():
                    out[number] = part

                @pl.when(jnp.logical_not(first))
                def _():
                    out[number] += part

            @pl.when(buffers[number] == 0)
            def _():
                add(own[:, column])

            @pl.when(buffers[number] > 0)
            def _():
                add(held[jnp.maximum(buffers[number] - 1, 0), :, column])

            return inner_carry

        return lax.fori_loop(0, live[position], one_slot, carry)

    lax.fori_loop(0, bins, one_bin, 0)


def block_products(source_expr, target_expr, held, local_idx, live, cells):
    genes, width = source_expr.shape
    bins, slots = local_idx.shape
    rows = max(size for size in range(8, 257, 8) if genes % size == 0)
    relative = local_idx // bins
    buffers = slot_of(lax.rem(lax.axis_index("tile"), GROUP), relative)
    columns = (local_idx - relative * bins) * cells
    smem = pl.BlockSpec(memory_space=pltpu.SMEM)
    out = pl.pallas_call(
        functools.partial(products_kernel, bins, slots, cells),
        out_shape=jax.ShapeDtypeStruct((bins * slots, cells, cells), jnp.float32),
        grid=(genes // rows,),
        in_specs=[
            smem,
            smem,
            smem,
            pl.BlockSpec((rows, width), lambda step: (step, 0)),
            pl.BlockSpec((rows, width), lambda step: (step, 0)),
            pl.BlockSpec((3, rows, width), lambda step: (0, step, 0)),
        ],
        out_specs=pl.BlockSpec((bins * slots, cells, cells), lambda step: (0, 0, 0)),
        compiler_params=pltpu.CompilerParams(vmem_limit_bytes=VMEM_LIMIT),
    )(live, buffers.reshape(-1), columns.reshape(-1), source_expr, target_expr, held)
    return out.reshape(bins, slots, cells, cells)


def price_kernel(inner, left, right, out):
    slots = inner.shape[1]
    for slot in range(slots):
        gw = left[0, :, 0:1] * right[0, slot, 0:1, :]
        for d in range(1, 4):
            gw += left[0, :, d : d + 1] * right[0, slot, d : d + 1, :]
        out[0, slot] = (-inner[0, slot] / G + THETA * gw) / EPS


def prices(inner, left_rows, right_rows):
    bins, slots, cells, _ = inner.shape
    block = pl.BlockSpec((1, slots, cells, cells), lambda n: (n, 0, 0, 0))
    return pl.pallas_call(
        price_kernel,
        out_shape=jax.ShapeDtypeStruct(inner.shape, jnp.float32),
        grid=(bins,),
        in_specs=[
            block,
            pl.BlockSpec((1, cells, 4), lambda n: (n, 0, 0)),
            pl.BlockSpec((1, slots, 4, cells), lambda n: (n, 0, 0, 0)),
        ],
        out_specs=block,
    )(inner, left_rows, right_rows)


def sweep_kernel(slots, live, index, price, log_mass, right, left_out, part_out, top, total):
    bins, cells = log_mass.shape
    top[...] = jnp.full(top.shape, MINUS_HUGE, jnp.float32)
    total[...] = jnp.zeros(total.shape, jnp.float32)

    def one_bin(position, carry):
        count = live[position]

        def right_of(slot):
            return right[pl.ds(index[position * slots + slot], 1), :]

        def best(slot, seen):
            return jnp.maximum(seen, right_of(slot) - price[position * slots + slot])

        seen = lax.fori_loop(1, count, best, right_of(0) - price[position * slots])
        peak = jnp.max(seen, axis=1, keepdims=True)

        def add(slot, mass):
            return mass + jnp.exp((right_of(slot) - price[position * slots + slot]) - peak)

        mass = lax.fori_loop(0, count, add, jnp.zeros((cells, cells), jnp.float32))
        spread = jnp.broadcast_to(log_mass[pl.ds(position, 1), :], (cells, cells))
        level = peak + jnp.log(jnp.sum(mass, axis=1, keepdims=True))
        left = jnp.transpose(spread)[:, 0:1] - level
        left_out[pl.ds(position, 1), :] = jnp.transpose(jnp.broadcast_to(left, (cells, cells)))[0:1, :]

        def column(slot, inner_carry):
            where = pl.ds(index[position * slots + slot], 1)
            rating = left - price[position * slots + slot]
            high = jnp.max(rating, axis=0, keepdims=True)
            amount = jnp.sum(jnp.exp(rating - high), axis=0, keepdims=True)
            held = top[where, :]
            both = jnp.maximum(held, high)
            total[where, :] = total[where, :] * jnp.exp(held - both) + amount * jnp.exp(high - both)
            top[where, :] = both
            return inner_carry

        return lax.fori_loop(0, count, column, carry)

    lax.fori_loop(0, bins, one_bin, 0)
    some = total[...] > 0
    part_out[...] = jnp.where(
        some, top[...] + jnp.log(jnp.where(some, total[...], 1.0)), MINUS_HUGE
    )


def sweep(live, index, price, log_mass, right):
    bins, slots = index.shape
    window, cells = right.shape
    smem, vmem = pl.BlockSpec(memory_space=pltpu.SMEM), pl.BlockSpec(memory_space=pltpu.VMEM)
    return pl.pallas_call(
        functools.partial(sweep_kernel, slots),
        out_shape=(
            jax.ShapeDtypeStruct((bins, cells), jnp.float32),
            jax.ShapeDtypeStruct((window, cells), jnp.float32),
        ),
        in_specs=[smem, smem, vmem, vmem, vmem],
        out_specs=(vmem, vmem),
        scratch_shapes=[pltpu.VMEM((window, cells), jnp.float32)] * 2,
        compiler_params=pltpu.CompilerParams(vmem_limit_bytes=VMEM_LIMIT),
    )(live, index.reshape(-1), price, log_mass, right)


def merge_kernel(tiles, cores, bins, part, log_mass, right, got, send_sem, recv_sem):
    me, core = lax.axis_index("tile"), lax.axis_index("gene")
    got[...] = jnp.full(got.shape, MINUS_HUGE, jnp.float32)
    barrier = pltpu.get_barrier_semaphore()
    others = []
    for shift in (-2, -1, 0, 1, 2):
        for turn in range(cores):
            if (shift, turn) != (0, 0):
                others.append((len(others), shift, turn))

    def guarded(shift, action):
        if shift == 0:
            action()
        else:
            pl.when((me + shift >= 0) & (me + shift < tiles))(action)

    def peer(shift, turn):
        return {"tile": me + shift, "gene": lax.rem(core + turn, cores)}

    for _, shift, turn in others:

        def greet(shift=shift, turn=turn):
            pl.semaphore_signal(barrier, inc=1, device_id=peer(shift, turn), device_id_type=MESH)

        guarded(shift, greet)
    present = sum(
        ((me + shift >= 0) & (me + shift < tiles)).astype(jnp.int32) for shift in (-2, -1, 1, 2)
    )
    pl.semaphore_wait(barrier, cores - 1 + cores * present)

    numbers = {(shift, turn): number for number, shift, turn in others}

    def rows_of(shift):
        return {-2: (0, bins), 2: (2 * bins, bins)}.get(shift, (0, 3 * bins))

    def copy(number, shift, turn):
        at, rows = rows_of(shift)
        back = numbers[(-shift, (cores - turn) % cores)]
        return pltpu.make_async_remote_copy(
            src_ref=part.at[pl.ds(at, rows), :],
            dst_ref=got.at[back, pl.ds(at, rows), :],
            send_sem=send_sem.at[number],
            recv_sem=recv_sem.at[back],
            device_id=peer(shift, turn),
            device_id_type=MESH,
        )

    def landing(number, shift, turn):
        at, rows = rows_of(-shift)
        return pltpu.make_async_remote_copy(
            src_ref=part.at[pl.ds(at, rows), :],
            dst_ref=got.at[number, pl.ds(at, rows), :],
            send_sem=send_sem.at[number],
            recv_sem=recv_sem.at[number],
            device_id=peer(shift, turn),
            device_id_type=MESH,
        )

    for number, shift, turn in others:
        guarded(shift, lambda n=number, s=shift, t=turn: copy(n, s, t).start())
    for number, shift, turn in others:
        guarded(shift, lambda n=number, s=shift, t=turn: landing(n, s, t).wait_recv())

    for place in range(3):
        here = place - 1
        parts = [part[place * bins : (place + 1) * bins, :]]
        for number, shift, turn in others:
            row = here - shift + 1
            if 0 <= row < 3:
                parts.append(got[number, row * bins : (row + 1) * bins, :])
        peak = functools.reduce(jnp.maximum, parts)
        mass = functools.reduce(jnp.add, [jnp.exp(one - peak) for one in parts])
        right[place * bins : (place + 1) * bins, :] = log_mass[
            place * bins : (place + 1) * bins, :
        ] - (peak + jnp.log(mass))

    for number, shift, turn in others:
        guarded(shift, lambda n=number, s=shift, t=turn: copy(n, s, t).wait_send())


def merge(part, log_mass, tiles, cores, bins):
    vmem = pl.BlockSpec(memory_space=pltpu.VMEM)
    count = 5 * cores - 1
    return pl.pallas_call(
        functools.partial(merge_kernel, tiles, cores, bins),
        out_shape=jax.ShapeDtypeStruct(part.shape, jnp.float32),
        in_specs=[vmem, vmem],
        out_specs=vmem,
        scratch_shapes=[
            pltpu.VMEM((count,) + part.shape, jnp.float32),
            pltpu.SemaphoreType.DMA((count,)),
            pltpu.SemaphoreType.DMA((count,)),
        ],
        compiler_params=pltpu.CompilerParams(collective_id=1, has_side_effects=True),
    )(part, log_mass)


def shards(
    source_expr,
    target_expr,
    prior_plan,
    nonzero_pattern,
    live,
    source_mass,
    target_mass,
    initial_logarithm_right,
):
    groups_on_chip_share, slots, spot_items = (
        prior_plan.shape[0],
        prior_plan.shape[1],
        prior_plan.shape[2],
    )
    tile_count = lax.axis_size("tile")
    tile_pos = lax.axis_index("tile")
    total_bins = groups_on_chip_share * tile_count
    panel_breadth = groups_on_chip_share * spot_items
    first_bin = tile_pos * groups_on_chip_share
    window_start = first_bin - groups_on_chip_share
    own_bins = first_bin + jnp.arange(groups_on_chip_share, dtype=jnp.int32)
    u_mom, u_dist = place_rows(own_bins, total_bins, spot_items)
    v_mom, v_dist = place_rows(nonzero_pattern, total_bins, spot_items)
    alive_indicator = jnp.arange(slots, dtype=jnp.int32)[None, :] < live[:, None]
    live_weight = alive_indicator.astype(jnp.float32)
    local_idx = nonzero_pattern - window_start
    gene_count = lax.axis_size("gene")
    gene_pos = lax.axis_index("gene")

    def pick(values):
        grouped = values.reshape(
            (groups_on_chip_share // gene_count, gene_count) + values.shape[1:]
        )
        return lax.dynamic_index_in_dim(grouped, gene_pos, 1, keepdims=False)

    share = jnp.sum(
        lax.map(block_moments, (pick(prior_plan), pick(u_mom), pick(v_mom), pick(live_weight))),
        axis=0,
    )
    moments = lax.psum(share, ("tile", "gene"))
    scaled = moments / moments[0, 0]
    held = halo_of(target_expr, tile_count)
    inner = block_products(source_expr, target_expr, held, local_idx, live, spot_items)
    inner = lax.psum_scatter(inner, "gene", scatter_dimension=0, tiled=True)
    share_bins = groups_on_chip_share // gene_count

    def half(values):
        return lax.dynamic_slice_in_dim(values, gene_pos * share_bins, share_bins, 0)

    left_rows = jnp.einsum("sid,de->sie", half(u_dist), scaled, precision=lax.Precision.HIGHEST)
    price = prices(inner, left_rows, jnp.swapaxes(half(v_dist), 2, 3))
    price = price.reshape(share_bins * slots, spot_items, spot_items)
    window_count = 3 * groups_on_chip_share
    both = with_halo(
        jnp.stack([initial_logarithm_right, target_mass]), (("tile", 1),), panel_breadth
    ).reshape(2, window_count, spot_items)
    right = both[0]
    log_target = jnp.log(jnp.where(both[1] > 0, both[1], 1.0))
    log_source = half(jnp.log(source_mass).reshape(groups_on_chip_share, spot_items))
    for step in range(ITERS):
        left, part = sweep(half(live), half(local_idx), price, log_source, right)
        right = merge(part, log_target, tile_count, gene_count, groups_on_chip_share)
    left = lax.all_gather(left, "gene", axis=0, tiled=True)
    own = right[groups_on_chip_share : 2 * groups_on_chip_share]
    return (left.reshape(-1), own.reshape(-1))


def solution(mesh):
    placed = (
        P("gene", "tile"),
        P("gene", "tile"),
        P("tile", None, None, None),
        P("tile", None),
        P("tile"),
        P("tile"),
        P("tile"),
        P("tile"),
    )
    return jax.shard_map(
        shards, mesh=mesh, in_specs=placed, out_specs=(P("tile"), P("tile")), check_vma=False
    )
```

```python
import functools

import jax
import jax.numpy as jnp
from jax import lax
from jax.experimental import pallas as pl
from jax.experimental.pallas import tpu as pltpu
from jax.sharding import PartitionSpec as P

G = 2000
ITERS = 3


EPS = 0.02
THETA = 0.1
MINUS_HUGE = -1e30


def with_halo(block, sides, width):
    for axis, dim in sides:
        count = lax.axis_size(axis)
        forward = [(i, i + 1) for i in range(count - 1)]
        backward = [(target, source) for source, target in forward]
        low = lax.ppermute(
            lax.slice_in_dim(block, block.shape[dim] - width, None, axis=dim), axis, forward
        )
        high = lax.ppermute(lax.slice_in_dim(block, 0, width, axis=dim), axis, backward)
        block = jnp.concatenate([low, block, high], axis=dim)
    return block


def place_rows(bins, nbins, spot_items):
    cell = jnp.arange(spot_items, dtype=jnp.int32)
    along = ((cell % 16).astype(jnp.float32) + 0.5) / 16.0
    xpos = (bins[..., None].astype(jnp.float32) + along) / nbins
    ypos = jnp.broadcast_to(((cell // 16).astype(jnp.float32) + 0.5) / (16.0 * nbins), xpos.shape)
    radius = xpos * xpos + ypos * ypos
    ones = jnp.ones_like(xpos)
    moment_rows = jnp.stack([ones, radius, xpos, ypos], axis=-1)
    dist_rows = jnp.stack([radius, ones, -2.0 * xpos, -2.0 * ypos], axis=-1)
    return (moment_rows, dist_rows)


def block_moments(args):
    plan, urow, vrow, weight = args
    plan_f = plan.astype(jnp.float32) * weight[:, None, None]
    pv = jnp.einsum("kij,kjd->kid", plan_f, vrow, precision=lax.Precision.HIGHEST)
    return jnp.einsum("ic,kid->cd", urow, pv, precision=lax.Precision.HIGHEST)


GROUP = 4
SEND_ROWS = 64
MESH = pl.DeviceIdType.MESH
VMEM_LIMIT = 60 * 1024 * 1024


def cuts_of(total, size):
    return [(at, min(size, total - at)) for at in range(0, total, size)]


def slot_of(rank, relative):
    low = jnp.where(rank == 0, 3, jnp.where(rank == 2, 2, 1))
    high = jnp.where(rank == 3, 3, jnp.where(rank == 1, 2, 1))
    return jnp.where(relative == 1, 0, jnp.where(relative == 0, low, high))


def halo_kernel(tiles, genes, tgt, held, send_sem, recv_sem):
    me = lax.axis_index("tile")
    rank = lax.rem(me, GROUP)
    across = {"tile": me + 1 - 2 * lax.rem(me, 2)}
    beside = {"tile": me + 2 - 4 * lax.rem(me // 2, 2)}
    edge = (rank == 0) | (rank == GROUP - 1)
    up = edge & (me + GROUP < tiles)
    down = edge & (me - GROUP >= 0)
    passes = ((rank == 0) & up) | ((rank == GROUP - 1) & down)
    gets = ((rank == 0) & down) | ((rank == GROUP - 1) & up)
    onward = {"tile": jnp.where(passes, jnp.where(rank == 0, me + GROUP, me - GROUP), me + 1 - 2 * lax.rem(me, 2))}

    barrier = pltpu.get_barrier_semaphore()
    pl.semaphore_signal(barrier, inc=1, device_id=across, device_id_type=MESH)
    pl.semaphore_signal(barrier, inc=1, device_id=beside, device_id_type=MESH)

    @pl.when(up)
    def _():
        pl.semaphore_signal(barrier, inc=1, device_id={"tile": me + GROUP}, device_id_type=MESH)

    @pl.when(down)
    def _():
        pl.semaphore_signal(barrier, inc=1, device_id={"tile": me - GROUP}, device_id_type=MESH)

    pl.semaphore_wait(barrier, 2 + up.astype(jnp.int32) + down.astype(jnp.int32))

    sends = cuts_of(genes, SEND_ROWS)

    def place(number, slot):
        at, rows = sends[number]
        return held.at[slot, pl.ds(at, rows), :]

    def copy(number, hop):
        at, rows = sends[number]
        return pltpu.make_async_remote_copy(
            src_ref=tgt.at[pl.ds(at, rows), :] if hop == 0 else place(number, hop - 1),
            dst_ref=place(number, hop),
            send_sem=send_sem.at[number, hop],
            recv_sem=recv_sem.at[number, hop],
            device_id=(across, beside, onward)[hop],
            device_id_type=MESH,
        )

    count = len(sends)
    for number in range(count):
        copy(number, 0).start()
    for step in range(count + 1):
        if step < count:
            copy(step, 0).wait_recv()
            copy(step, 1).start()
        if step >= 1:
            copy(step - 1, 1).wait_recv()

            @pl.when(passes)
            def _(step=step):
                copy(step - 1, 2).start()

    @pl.when(gets)
    def _():
        for number in range(count):
            copy(number, 2).wait_recv()

    for number in range(count):
        copy(number, 0).wait_send()
        copy(number, 1).wait_send()

    @pl.when(passes)
    def _():
        for number in range(count):
            copy(number, 2).wait_send()


def halo_of(target_expr, tiles):
    genes, width = target_expr.shape
    count = len(cuts_of(genes, SEND_ROWS))
    return pl.pallas_call(
        functools.partial(halo_kernel, tiles, genes),
        out_shape=jax.ShapeDtypeStruct((3, genes, width), target_expr.dtype),
        in_specs=[pl.BlockSpec(memory_space=pl.ANY)],
        out_specs=pl.BlockSpec(memory_space=pl.ANY),
        scratch_shapes=[pltpu.SemaphoreType.DMA((count, 3)), pltpu.SemaphoreType.DMA((count, 3))],
        compiler_params=pltpu.CompilerParams(collective_id=0, has_side_effects=True),
    )(target_expr)


def products_kernel(bins, slots, cells, live, buffers, columns, src, own, held, out, turned, window, sems):
    genes = own.shape[0]
    copies = [pltpu.make_async_copy(own, window.at[0], sems.at[0])] + [
        pltpu.make_async_copy(held.at[slot], window.at[slot + 1], sems.at[slot + 1]) for slot in range(3)
    ]
    for one in copies:
        one.start()

    def turn(position, carry):
        block = src[:, pl.ds(pl.multiple_of(position * cells, cells), cells)]
        turned[position] = jnp.transpose(block)
        return carry

    lax.fori_loop(0, bins, turn, 0)
    for one in copies:
        one.wait()

    def one_bin(position, carry):
        def one_pair(pair, inner_carry):
            number = position * slots + 2 * pair

            def other(which):
                column = pl.ds(pl.multiple_of(columns[which], cells), cells)
                return window[buffers[which], :, column]

            part = jnp.dot(
                turned[position],
                jnp.concatenate([other(number), other(number + 1)], axis=1),
                preferred_element_type=jnp.float32,
            )
            out[number] = part[:, :cells]
            out[number + 1] = part[:, cells:]
            return inner_carry

        return lax.fori_loop(0, (live[position] + 1) // 2, one_pair, carry)

    lax.fori_loop(0, bins, one_bin, 0)


def block_products(source_expr, target_expr, held, local_idx, live, cells):
    genes, width = source_expr.shape
    bins, slots = local_idx.shape
    relative = local_idx // bins
    buffers = slot_of(lax.rem(lax.axis_index("tile"), GROUP), relative)
    columns = (local_idx - relative * bins) * cells
    smem, vmem = pl.BlockSpec(memory_space=pltpu.SMEM), pl.BlockSpec(memory_space=pltpu.VMEM)
    anywhere = pl.BlockSpec(memory_space=pl.ANY)
    return pl.pallas_call(
        functools.partial(products_kernel, bins, slots, cells),
        out_shape=jax.ShapeDtypeStruct((bins * slots, cells, cells), jnp.float32),
        in_specs=[smem, smem, smem, vmem, anywhere, anywhere],
        out_specs=vmem,
        scratch_shapes=[
            pltpu.VMEM((bins, cells, genes), source_expr.dtype),
            pltpu.VMEM((4, genes, width), target_expr.dtype),
            pltpu.SemaphoreType.DMA((4,)),
        ],
        compiler_params=pltpu.CompilerParams(vmem_limit_bytes=VMEM_LIMIT),
    )(live, buffers.reshape(-1), columns.reshape(-1), source_expr, target_expr, held)


EXCHANGES = 8


def exchange_kernel(inner, out, send_sem, recv_sem):
    core = lax.axis_index("gene")
    other = {"gene": 1 - core}
    barrier = pltpu.get_barrier_semaphore()
    pl.semaphore_signal(barrier, inc=1, device_id=other, device_id_type=MESH)
    pl.semaphore_wait(barrier, 1)
    half = out.shape[0]
    piece = half // EXCHANGES
    copies = [
        pltpu.make_async_remote_copy(
            src_ref=inner.at[pl.ds((1 - core) * half + at * piece, piece)],
            dst_ref=out.at[pl.ds(at * piece, piece)],
            send_sem=send_sem.at[at],
            recv_sem=recv_sem.at[at],
            device_id=other,
            device_id_type=MESH,
        )
        for at in range(EXCHANGES)
    ]
    for one in copies:
        one.start()
    for one in copies:
        one.wait()


def exchange(inner):
    anywhere = pl.BlockSpec(memory_space=pl.ANY)
    return pl.pallas_call(
        exchange_kernel,
        out_shape=jax.ShapeDtypeStruct((inner.shape[0] // 2,) + inner.shape[1:], inner.dtype),
        in_specs=[anywhere],
        out_specs=anywhere,
        scratch_shapes=[
            pltpu.SemaphoreType.DMA((EXCHANGES,)),
            pltpu.SemaphoreType.DMA((EXCHANGES,)),
        ],
        compiler_params=pltpu.CompilerParams(collective_id=2, has_side_effects=True),
    )(inner)


def price_kernel(core, mine, other, left, right, out):
    slots = mine.shape[0]
    scaled = left[0] * (THETA / EPS)
    for slot in range(slots):
        value = (mine[slot] + other[slot]) * (-1.0 / (G * EPS))
        for d in range(4):
            value += scaled[:, d : d + 1] * right[0, slot, d : d + 1, :]
        out[slot] = value


def prices(inner, other, core, left_rows, right_rows):
    bins, slots, _, cells = right_rows.shape
    block = pl.BlockSpec((slots, cells, cells), lambda n, core: (n, 0, 0))
    return pl.pallas_call(
        price_kernel,
        out_shape=jax.ShapeDtypeStruct(other.shape, jnp.float32),
        grid_spec=pltpu.PrefetchScalarGridSpec(
            num_scalar_prefetch=1,
            grid=(bins,),
            in_specs=[
                pl.BlockSpec((slots, cells, cells), lambda n, core: (core[0] * bins + n, 0, 0)),
                block,
                pl.BlockSpec((1, cells, 4), lambda n, core: (n, 0, 0)),
                pl.BlockSpec((1, slots, 4, cells), lambda n, core: (n, 0, 0, 0)),
            ],
            out_specs=block,
        ),
    )(core.reshape(1), inner, other, left_rows, right_rows)


def sweep_kernel(slots, live, index, price, log_mass, right, left_out, part_out, top, total):
    bins, cells = log_mass.shape
    top[...] = jnp.full(top.shape, MINUS_HUGE, jnp.float32)
    total[...] = jnp.zeros(total.shape, jnp.float32)

    def one_bin(position, carry):
        count = live[position]

        def right_of(slot):
            return right[pl.ds(index[position * slots + slot], 1), :]

        def best(slot, seen):
            return jnp.maximum(seen, right_of(slot) - price[position * slots + slot])

        seen = lax.fori_loop(1, count, best, right_of(0) - price[position * slots])
        peak = jnp.max(seen, axis=1, keepdims=True)

        def add(slot, mass):
            return mass + jnp.exp((right_of(slot) - price[position * slots + slot]) - peak)

        mass = lax.fori_loop(0, count, add, jnp.zeros((cells, cells), jnp.float32))
        spread = jnp.broadcast_to(log_mass[pl.ds(position, 1), :], (cells, cells))
        level = peak + jnp.log(jnp.sum(mass, axis=1, keepdims=True))
        left = jnp.transpose(spread)[:, 0:1] - level
        left_out[pl.ds(position, 1), :] = jnp.transpose(jnp.broadcast_to(left, (cells, cells)))[0:1, :]

        def column(slot, inner_carry):
            where = pl.ds(index[position * slots + slot], 1)
            rating = left - price[position * slots + slot]
            high = jnp.max(rating, axis=0, keepdims=True)
            amount = jnp.sum(jnp.exp(rating - high), axis=0, keepdims=True)
            held = top[where, :]
            both = jnp.maximum(held, high)
            total[where, :] = total[where, :] * jnp.exp(held - both) + amount * jnp.exp(high - both)
            top[where, :] = both
            return inner_carry

        return lax.fori_loop(0, count, column, carry)

    lax.fori_loop(0, bins, one_bin, 0)
    some = total[...] > 0
    part_out[...] = jnp.where(
        some, top[...] + jnp.log(jnp.where(some, total[...], 1.0)), MINUS_HUGE
    )


def sweep(live, index, price, log_mass, right):
    bins, slots = index.shape
    window, cells = right.shape
    smem, vmem = pl.BlockSpec(memory_space=pltpu.SMEM), pl.BlockSpec(memory_space=pltpu.VMEM)
    return pl.pallas_call(
        functools.partial(sweep_kernel, slots),
        out_shape=(
            jax.ShapeDtypeStruct((bins, cells), jnp.float32),
            jax.ShapeDtypeStruct((window, cells), jnp.float32),
        ),
        in_specs=[smem, smem, vmem, vmem, vmem],
        out_specs=(vmem, vmem),
        scratch_shapes=[pltpu.VMEM((window, cells), jnp.float32)] * 2,
        compiler_params=pltpu.CompilerParams(vmem_limit_bytes=VMEM_LIMIT),
    )(live, index.reshape(-1), price, log_mass, right)


def merge_kernel(tiles, cores, bins, part, log_mass, right, got, send_sem, recv_sem):
    me, core = lax.axis_index("tile"), lax.axis_index("gene")
    got[...] = jnp.full(got.shape, MINUS_HUGE, jnp.float32)
    barrier = pltpu.get_barrier_semaphore()
    others = []
    for shift in (-2, -1, 0, 1, 2):
        for turn in range(cores):
            if (shift, turn) != (0, 0):
                others.append((len(others), shift, turn))

    def guarded(shift, action):
        if shift == 0:
            action()
        else:
            pl.when((me + shift >= 0) & (me + shift < tiles))(action)

    def peer(shift, turn):
        return {"tile": me + shift, "gene": lax.rem(core + turn, cores)}

    for _, shift, turn in others:

        def greet(shift=shift, turn=turn):
            pl.semaphore_signal(barrier, inc=1, device_id=peer(shift, turn), device_id_type=MESH)

        guarded(shift, greet)
    present = sum(
        ((me + shift >= 0) & (me + shift < tiles)).astype(jnp.int32) for shift in (-2, -1, 1, 2)
    )
    pl.semaphore_wait(barrier, cores - 1 + cores * present)

    numbers = {(shift, turn): number for number, shift, turn in others}

    def rows_of(shift):
        return {-2: (0, bins), 2: (2 * bins, bins)}.get(shift, (0, 3 * bins))

    def copy(number, shift, turn):
        at, rows = rows_of(shift)
        back = numbers[(-shift, (cores - turn) % cores)]
        return pltpu.make_async_remote_copy(
            src_ref=part.at[pl.ds(at, rows), :],
            dst_ref=got.at[back, pl.ds(at, rows), :],
            send_sem=send_sem.at[number],
            recv_sem=recv_sem.at[back],
            device_id=peer(shift, turn),
            device_id_type=MESH,
        )

    def landing(number, shift, turn):
        at, rows = rows_of(-shift)
        return pltpu.make_async_remote_copy(
            src_ref=part.at[pl.ds(at, rows), :],
            dst_ref=got.at[number, pl.ds(at, rows), :],
            send_sem=send_sem.at[number],
            recv_sem=recv_sem.at[number],
            device_id=peer(shift, turn),
            device_id_type=MESH,
        )

    for number, shift, turn in others:
        guarded(shift, lambda n=number, s=shift, t=turn: copy(n, s, t).start())
    for number, shift, turn in others:
        guarded(shift, lambda n=number, s=shift, t=turn: landing(n, s, t).wait_recv())

    for place in range(3):
        here = place - 1
        parts = [part[place * bins : (place + 1) * bins, :]]
        for number, shift, turn in others:
            row = here - shift + 1
            if 0 <= row < 3:
                parts.append(got[number, row * bins : (row + 1) * bins, :])
        peak = functools.reduce(jnp.maximum, parts)
        mass = functools.reduce(jnp.add, [jnp.exp(one - peak) for one in parts])
        right[place * bins : (place + 1) * bins, :] = log_mass[
            place * bins : (place + 1) * bins, :
        ] - (peak + jnp.log(mass))

    for number, shift, turn in others:
        guarded(shift, lambda n=number, s=shift, t=turn: copy(n, s, t).wait_send())


def merge(part, log_mass, tiles, cores, bins):
    vmem = pl.BlockSpec(memory_space=pltpu.VMEM)
    count = 5 * cores - 1
    return pl.pallas_call(
        functools.partial(merge_kernel, tiles, cores, bins),
        out_shape=jax.ShapeDtypeStruct(part.shape, jnp.float32),
        in_specs=[vmem, vmem],
        out_specs=vmem,
        scratch_shapes=[
            pltpu.VMEM((count,) + part.shape, jnp.float32),
            pltpu.SemaphoreType.DMA((count,)),
            pltpu.SemaphoreType.DMA((count,)),
        ],
        compiler_params=pltpu.CompilerParams(collective_id=1, has_side_effects=True),
    )(part, log_mass)


def shards(
    source_expr,
    target_expr,
    prior_plan,
    nonzero_pattern,
    live,
    source_mass,
    target_mass,
    initial_logarithm_right,
):
    groups_on_chip_share, slots, spot_items = (
        prior_plan.shape[0],
        prior_plan.shape[1],
        prior_plan.shape[2],
    )
    tile_count = lax.axis_size("tile")
    tile_pos = lax.axis_index("tile")
    total_bins = groups_on_chip_share * tile_count
    panel_breadth = groups_on_chip_share * spot_items
    first_bin = tile_pos * groups_on_chip_share
    window_start = first_bin - groups_on_chip_share
    own_bins = first_bin + jnp.arange(groups_on_chip_share, dtype=jnp.int32)
    u_mom, u_dist = place_rows(own_bins, total_bins, spot_items)
    v_mom, v_dist = place_rows(nonzero_pattern, total_bins, spot_items)
    alive_indicator = jnp.arange(slots, dtype=jnp.int32)[None, :] < live[:, None]
    live_weight = alive_indicator.astype(jnp.float32)
    local_idx = nonzero_pattern - window_start
    gene_count = lax.axis_size("gene")
    gene_pos = lax.axis_index("gene")

    def pick(values):
        grouped = values.reshape(
            (groups_on_chip_share // gene_count, gene_count) + values.shape[1:]
        )
        return lax.dynamic_index_in_dim(grouped, gene_pos, 1, keepdims=False)

    share = jnp.sum(
        lax.map(block_moments, (pick(prior_plan), pick(u_mom), pick(v_mom), pick(live_weight))),
        axis=0,
    )
    moments = lax.psum(share, ("tile", "gene"))
    scaled = moments / moments[0, 0]
    held = halo_of(target_expr, tile_count)
    inner = block_products(source_expr, target_expr, held, local_idx, live, spot_items)
    other = exchange(inner)
    share_bins = groups_on_chip_share // gene_count

    def half(values):
        return lax.dynamic_slice_in_dim(values, gene_pos * share_bins, share_bins, 0)

    left_rows = jnp.einsum("sid,de->sie", half(u_dist), scaled, precision=lax.Precision.HIGHEST)
    price = prices(inner, other, gene_pos, left_rows, jnp.swapaxes(half(v_dist), 2, 3))
    window_count = 3 * groups_on_chip_share
    both = with_halo(
        jnp.stack([initial_logarithm_right, target_mass]), (("tile", 1),), panel_breadth
    ).reshape(2, window_count, spot_items)
    right = both[0]
    log_target = jnp.log(jnp.where(both[1] > 0, both[1], 1.0))
    log_source = half(jnp.log(source_mass).reshape(groups_on_chip_share, spot_items))
    for step in range(ITERS):
        left, part = sweep(half(live), half(local_idx), price, log_source, right)
        right = merge(part, log_target, tile_count, gene_count, groups_on_chip_share)
    left = lax.all_gather(left, "gene", axis=0, tiled=True)
    own = right[groups_on_chip_share : 2 * groups_on_chip_share]
    return (left.reshape(-1), own.reshape(-1))


def solution(mesh):
    placed = (
        P("gene", "tile"),
        P("gene", "tile"),
        P("tile", None, None, None),
        P("tile", None),
        P("tile"),
        P("tile"),
        P("tile"),
        P("tile"),
    )
    return jax.shard_map(
        shards, mesh=mesh, in_specs=placed, out_specs=(P("tile"), P("tile")), check_vma=False
    )
```
